32 devices in a mesh: expert: 4 (over y, x), etp: 8 (over z, core).
Axes of the slice: x: 2, y: 2, z: 4, core: 2. Of those that a mesh axis runs over, the one named last changes fastest.
Arguments:
- tokens: bfloat16 [512, 2880], P('expert', 'etp'), may hold values from -6 to 6
- grad_out: bfloat16 [512, 2880], P('expert', 'etp'), may hold values from -6 to 6
- gates: float32 [512, 4], P('expert'), may hold values from 0.05 to 0.6
- routes: int32 [512, 4], P('expert'), may hold values from 0 to 7, all different within a row; in each aligned block of 128 rows (0 to 127, 128 to 255, ...) at most 96 rows name the same one
- w_gate: bfloat16 [8, 2880, 2880], P('expert', 'etp'), may hold values from -0.109375 to 0.109375
- w_up: bfloat16 [8, 2880, 2880], P('expert', 'etp'), may hold values from -0.109375 to 0.109375
- w_down: bfloat16 [8, 2880, 2880], P('expert', 'etp'), may hold values from -0.109375 to 0.109375
Outputs:
- d_tokens: bfloat16 [512, 2880], P('expert', 'etp')
- d_gate: bfloat16 [8, 2880, 2880], P('expert', 'etp')
- d_up: bfloat16 [8, 2880, 2880], P('expert', 'etp')
- d_down: bfloat16 [8, 2880, 2880], P('expert', 'etp')
The draws below stay inside these ranges and needn't reach their ends.
Inputs may be any that keep to these rules, and one draw needn't show every extreme that they name: `routes`: each row names 4 different experts. In each aligned block of 128 rows (the tokens of one index of expert) no expert is named by more than 96 rows, and in some block one expert is named by exactly 96 rows.
All inputs are finite; a program needn't handle non-finite values.
Results may differ from the reference program's by a relative error of at most 0.0058.
Values may be sent and summed in bfloat16 or wider, within the bound.
No kernel may reach another device: no remote copies, remote signals or barrier semaphores. Data moves between devices by JAX's collectives and lax.ppermute only.
A program may use at most 128 MiB of HBM per device.

```python
import math
import jax
import jax.numpy as jnp
import numpy as np
from jax import lax

D = 2880
FF = 2880
TOPK = 4
TOK_DEV = 128
EXPERTS = 8
TOKENS = 512
CAP = 96
N_EXPERT = 4


def levels(key, extent, shards, low, top_value):
    gain = 1.0
    for position, shards_of in shards:
        steps = jax.random.uniform(jax.random.fold_in(jax.random.fold_in(key, 6), position), (shards_of,), jnp.float32, low / len(shards), top_value / len(shards))
        gain = gain * jnp.repeat(jnp.exp(steps), extent[position] // shards_of).reshape((-1,) + (1,) * (len(extent) - 1 - position))
    return gain


def shared_out(rng, own, number, rows, number_of, top, most, skew):
    sequence = jax.random.permutation(rng, number_of)
    packed, usual = load_shares(number_of, rows * top, most, skew, True), load_shares(number_of, rows * top, most, skew, False)
    places = jnp.arange(number_of)

    def named(tallies, offset_by):
        used = int((tallies > 0).sum())
        fixed = max(1, used // 4)
        moved = fixed + (places - fixed + offset_by * (used - fixed)) % max(1, number_of - fixed)
        return jnp.zeros((number_of,), jnp.int32).at[sequence[jnp.where(places < fixed, places, moved)]].set(jnp.asarray(tallies, jnp.int32))

    tallies = jnp.where(number % 4 == 0, named(packed, number // 4), named(usual, number - number // 4 - 1))
    mixed = jax.random.permutation(jax.random.fold_in(own, 3), number_of)
    giver, taker = mixed[0:number_of // 2 * 2:2], mixed[1:number_of // 2 * 2:2]
    margin = jnp.minimum(tallies[giver] - 1, most - tallies[taker]) // 2
    margin = jnp.where((giver == sequence[0]) | (taker == sequence[0]) | (tallies[taker] == 0), 0, jnp.maximum(margin, 0))
    moved = jax.random.randint(jax.random.fold_in(own, 4), (number_of // 2,), 0, 1 << 20) % (margin + 1)
    tallies = tallies.at[giver].add(-moved).at[taker].add(moved)
    items = jnp.searchsorted(jnp.cumsum(tallies), jnp.arange(rows * top), side="right").astype(jnp.int32)
    listing = items.reshape(top, rows).T
    listing = listing[jax.random.permutation(jax.random.fold_in(own, 1), rows)]
    offset_by = jax.random.randint(jax.random.fold_in(own, 2), (rows, 1), 0, top)
    return jnp.take_along_axis(listing, (jnp.arange(top)[None, :] + offset_by) % top, axis=1)


def load_shares(number_of, total, limit, skew, full):
    weights = [(1 << 20) // math.isqrt(rank ** skew) + 1 for rank in range(1, number_of + 1)]
    largest = limit if full else min(limit, max(-(-total // number_of), total * weights[0] // sum(weights)))
    least = 1 if total - largest >= number_of - 1 else 0
    counts, spare = [largest] + [least] * (number_of - 1), total - largest - least * (number_of - 1)
    while spare > 0:
        candidates = [i for i in range(1, number_of) if counts[i] < largest] or [i for i in range(1, number_of) if counts[i] < limit]
        mass, budget = sum([weights[i] for i in candidates]), spare
        for i in candidates:
            extra = min(limit - counts[i], max(1, budget * weights[i] // mass), spare)
            counts[i] = counts[i] + extra
            spare = spare - extra
    return np.array(counts)


def centred(key, extent, spread, limit, shards=(), kind=jnp.bfloat16):
    result = jax.random.normal(key, extent, jnp.float32) * spread
    if len(shards) > 0:
        result = levels(key, extent, shards, -0.22, 0.18) * result
    return jnp.clip(result, min=-limit, max=limit).astype(kind)


def setup_inputs(seed: int = 0) -> dict:
    keys = jax.random.split(jax.random.key(seed), 8)
    tokens = centred(keys[0], (TOKENS, D), 1.0, 6.0, ((0, 4), (1, 8)))
    grad_out = centred(keys[1], (TOKENS, D), 1.0, 6.0, ((0, 4), (1, 8)))
    gates = jnp.clip(jnp.exp(math.log(0.6) - 2.4849067 * jax.random.uniform(keys[2], (TOKENS, TOPK), jnp.float32) ** levels(keys[2], (TOKENS, TOPK), ((0, 4),), -0.2, 0.2)), 0.05, 0.6)
    routes_keys = jax.random.split(jax.random.fold_in(keys[3], 1), TOKENS // TOK_DEV)
    routes_turns = jax.random.permutation(jax.random.fold_in(keys[3], 3), TOKENS // TOK_DEV)
    routes = jax.vmap(lambda own, number: shared_out(jax.random.fold_in(keys[3], 2), own, number, TOK_DEV, EXPERTS, TOPK, CAP, 2))(routes_keys, routes_turns).reshape((TOKENS, TOPK))
    w_gate = centred(keys[4], (EXPERTS, FF, D), D ** -0.5, 0.109375, ((0, 4), (1, 8)))
    w_up = centred(keys[5], (EXPERTS, FF, D), D ** -0.5, 0.109375, ((0, 4), (1, 8)))
    w_down = centred(keys[6], (EXPERTS, FF, D), FF ** -0.5, 0.109375, ((0, 4), (1, 8)))
    return dict(tokens=tokens, grad_out=grad_out, gates=gates, routes=routes, w_gate=w_gate, w_up=w_up, w_down=w_down)


def reference(tokens, grad_out, gates, routes, w_gate, w_up, w_down):
    pairs = TOKENS * TOPK
    rows = N_EXPERT * CAP
    flat = routes.reshape(-1)
    tok_index = (jnp.arange(pairs, dtype=jnp.int32) // TOPK).astype(jnp.int32)
    scaled = (gates.reshape(-1)[:, None] * grad_out[tok_index].astype(jnp.float32)).astype(jnp.bfloat16)

    def per_expert(carry, expert_id):
        order = jnp.argsort((flat != expert_id).astype(jnp.int32), stable=True)[:rows].astype(jnp.int32)
        valid = flat[order] == expert_id
        owners = (order // TOPK).astype(jnp.int32)
        x_rows = jnp.where(valid[:, None], tokens[owners], 0).astype(jnp.bfloat16)
        g_rows = jnp.where(valid[:, None], scaled[order], 0).astype(jnp.bfloat16)
        gate_w = w_gate[expert_id]
        up_w = w_up[expert_id]
        down_w = w_down[expert_id]
        pre_gate = jnp.dot(x_rows, gate_w.T, preferred_element_type=jnp.float32)
        pre_up = jnp.dot(x_rows, up_w.T, preferred_element_type=jnp.float32)
        d_act = jnp.dot(g_rows, down_w.T, preferred_element_type=jnp.float32)
        sig = jax.nn.sigmoid(1.702 * pre_gate)
        glu = pre_gate * sig
        act = (glu * (pre_up + 1.0)).astype(jnp.bfloat16)
        d_pre_gate = (d_act * (pre_up + 1.0) * (sig + 1.702 * pre_gate * sig * (1.0 - sig))).astype(jnp.bfloat16)
        d_pre_up = (d_act * glu).astype(jnp.bfloat16)
        grad_gate = jnp.dot(d_pre_gate.T, x_rows, preferred_element_type=jnp.float32).astype(jnp.bfloat16)
        grad_up = jnp.dot(d_pre_up.T, x_rows, preferred_element_type=jnp.float32).astype(jnp.bfloat16)
        grad_down = jnp.dot(act.T, g_rows, preferred_element_type=jnp.float32).astype(jnp.bfloat16)
        term = jnp.dot(d_pre_gate, gate_w, preferred_element_type=jnp.float32)
        term = term + jnp.dot(d_pre_up, up_w, preferred_element_type=jnp.float32)
        carry = carry.at[owners].add(jnp.where(valid[:, None], term, jnp.float32(0.0)))
        return carry, (grad_gate, grad_up, grad_down)

    start = jnp.zeros((TOKENS, D), jnp.float32)
    total, grads = lax.scan(per_expert, start, jnp.arange(EXPERTS, dtype=jnp.int32))
    return total.astype(jnp.bfloat16), grads[0], grads[1], grads[2]
```

```python
import jax
import jax.numpy as jnp
from jax import lax
from jax.sharding import Mesh
from jax.sharding import PartitionSpec as P

BF16, F32 = jnp.bfloat16, jnp.float32


def xor_send(a, axis, s):
    return lax.ppermute(a, axis, [(i, i ^ s) for i in range(lax.axis_size(axis))])


def gather_columns(own):
    rings = lax.all_gather(own, "ring", axis=0)
    blocks = [rings] + [
        xor_send(rings, "expert", s) for s in range(1, lax.axis_size("expert"))
    ]
    half = jnp.concatenate(blocks, -1)
    other = xor_send(half, "core", 1)
    first = lax.axis_index("core") == 0
    both = jnp.where(first, jnp.stack([half, other], 1), jnp.stack([other, half], 1))
    return both.reshape(-1, both.shape[-1])


def sum_home(part, rows):
    rings, groups = lax.axis_size("ring"), lax.axis_size("expert")
    core, ring = lax.axis_index("core"), lax.axis_index("ring")
    part = part.reshape(rings, 2, -1, part.shape[-1])
    keep = lax.dynamic_index_in_dim(part, core, 1, False)
    give = lax.dynamic_index_in_dim(part, 1 - core, 1, False).astype(BF16)
    chip = keep + xor_send(give, "core", 1).astype(F32)
    chip_b = chip.astype(BF16)
    mine = chip[..., :rows]
    for s in range(1, groups):
        mine = mine + xor_send(chip_b[..., s * rows : (s + 1) * rows], "expert", s).astype(F32)
    mine_b = mine.astype(BF16)
    home = lax.dynamic_index_in_dim(mine, ring, 0, False)
    for s in range(1, rings):
        home = home + xor_send(
            lax.dynamic_index_in_dim(mine_b, ring ^ s, 0, False), "ring", s
        ).astype(F32)
    return home.astype(BF16)


def body(tokens, grad_out, gates, routes, w_gate, w_up, w_down):
    groups = lax.axis_size("expert")
    local = w_gate.shape[0]
    rows = tokens.shape[0]
    group = lax.axis_index("expert")

    ids = jnp.arange(groups * local, dtype=jnp.int32)
    named = routes[None] == ids[:, None, None]
    weight = jnp.sum(jnp.where(named, gates[None], 0.0), -1)
    weight = weight.reshape(groups, local, rows)
    coef = [lax.dynamic_index_in_dim(weight, group, 0, False)]
    for s in range(1, groups):
        coef.append(xor_send(lax.dynamic_index_in_dim(weight, group ^ s, 0, False), "expert", s))
    coef = jnp.concatenate(coef, -1)[:, None, :]

    x = gather_columns(tokens.T)
    g = gather_columns(grad_out.T)

    def to_hidden(w, a):
        return jnp.einsum("efd,dt->eft", w, a, preferred_element_type=F32)

    pre_gate = to_hidden(w_gate, x)
    pre_up = to_hidden(w_up, x)
    d_act = to_hidden(w_down, g) * coef
    sig = jax.nn.sigmoid(1.702 * pre_gate)
    glu = pre_gate * sig
    act = (glu * (pre_up + 1.0) * coef).astype(BF16)
    d_pre_gate = (d_act * (pre_up + 1.0) * (sig + 1.702 * pre_gate * sig * (1.0 - sig))).astype(BF16)
    d_pre_up = (d_act * glu).astype(BF16)

    term = jnp.einsum("efd,eft->dt", w_gate, d_pre_gate, preferred_element_type=F32)
    term = term + jnp.einsum("efd,eft->dt", w_up, d_pre_up, preferred_element_type=F32)
    d_tokens = sum_home(term, rows).T

    def to_weight(a, b):
        return jnp.einsum("eft,dt->efd", a, b, preferred_element_type=F32).astype(BF16)

    return d_tokens, to_weight(d_pre_gate, x), to_weight(d_pre_up, x), to_weight(act, g)


def solution(mesh):
    groups, shards = mesh.shape["expert"], mesh.shape["etp"]
    split = Mesh(mesh.devices.reshape(groups, shards // 2, 2), ("expert", "ring", "core"))
    etp = ("ring", "core")
    hidden = P("expert", etp, None)
    return jax.shard_map(
        body,
        mesh=split,
        in_specs=(P("expert", etp), P("expert", etp), P("expert", None), P("expert", None), hidden, hidden, hidden),
        out_specs=(P("expert", etp), hidden, hidden, hidden),
        check_vma=False,
    )
```

```python
import jax
import jax.numpy as jnp
from jax import lax
from jax.sharding import Mesh
from jax.sharding import PartitionSpec as P

BF16, F32 = jnp.bfloat16, jnp.float32


def xor_send(a, axis, s):
    return lax.ppermute(a, axis, [(i, i ^ s) for i in range(lax.axis_size(axis))])


def ring_order(pieces):
    ring, bit = lax.axis_index("ring"), 1
    while bit < len(pieces):
        swap = (ring & bit) > 0
        pieces = [jnp.where(swap, pieces[i ^ bit], pieces[i]) for i in range(len(pieces))]
        bit *= 2
    return jnp.stack(pieces)


def ring_gather(own):
    return [own] + [xor_send(own, "ring", s) for s in range(1, lax.axis_size("ring"))]


def plane_gather(a):
    return [a] + [xor_send(a, "expert", s) for s in range(1, lax.axis_size("expert"))]


def both_cores(half):
    other = xor_send(half, "core", 1)
    first = lax.axis_index("core") == 0
    both = jnp.where(first, jnp.stack([half, other], 1), jnp.stack([other, half], 1))
    return both.reshape(-1, both.shape[-1])


def at(a, i):
    return lax.dynamic_index_in_dim(a, i, 0, False)


def swap_sum(part):
    core = lax.axis_index("core")
    part = part.reshape(lax.axis_size("ring"), 2, -1, part.shape[-1])
    keep = lax.dynamic_index_in_dim(part, core, 1, False)
    give = lax.dynamic_index_in_dim(part, 1 - core, 1, False)
    return keep, xor_send(give, "core", 1)


def plane_sum(keep, other, rows):
    chip = keep.astype(F32) + other.astype(F32)
    far = chip[:, :, rows:].astype(BF16)
    arrived = [
        xor_send(far[:, :, (s - 1) * rows : s * rows], "expert", s)
        for s in range(1, lax.axis_size("expert"))
    ]
    return chip[:, :, :rows], arrived


def ring_sum(mine):
    ring = lax.axis_index("ring")
    mine_b = mine.astype(BF16)
    home = at(mine, ring)
    for s in range(1, lax.axis_size("ring")):
        home = home + xor_send(at(mine_b, ring ^ s), "ring", s).astype(F32)
    return home.astype(BF16)


def body(tokens, grad_out, gates, routes, w_gate, w_up, w_down):
    groups = lax.axis_size("expert")
    local = w_gate.shape[0]
    rows = tokens.shape[0]
    group = lax.axis_index("expert")

    ids = jnp.arange(groups * local, dtype=jnp.int32)
    named = routes[None] == ids[:, None, None]
    weight = jnp.sum(jnp.where(named, gates[None], 0.0), -1)
    weight = weight.reshape(groups, local, rows)
    coef = [at(weight, group)]
    for s in range(1, groups):
        coef.append(xor_send(at(weight, group ^ s), "expert", s))

    def to_hidden(w, a):
        return jnp.einsum("efd,dt->eft", w, a, preferred_element_type=F32)

    x_own, g_own = tokens.T, grad_out.T
    x_ring = ring_order(ring_gather(x_own))
    x_ring, coef, g_own = lax.optimization_barrier((x_ring, coef, g_own))
    x_blocks = plane_gather(x_ring)
    g_ring = lax.all_gather(g_own, "ring", axis=0)
    x_blocks, g_ring = lax.optimization_barrier((x_blocks, g_ring))
    g_blocks = plane_gather(g_ring)
    x = both_cores(jnp.concatenate(x_blocks, -1))
    coef = jnp.concatenate(coef, -1)[:, None, :]
    pre_gate = to_hidden(w_gate, x)
    pre_up = to_hidden(w_up, x)
    sig = jax.nn.sigmoid(1.702 * pre_gate)
    glu = pre_gate * sig
    act = (glu * (pre_up + 1.0) * coef).astype(BF16)
    slope = (pre_up + 1.0) * (sig + 1.702 * pre_gate * sig * (1.0 - sig))
    g_blocks, act, glu, slope = lax.optimization_barrier((g_blocks, act, glu, slope))
    g = both_cores(jnp.concatenate(g_blocks, -1))

    d_act = to_hidden(w_down, g) * coef
    d_pre_gate = (d_act * slope).astype(BF16)
    d_pre_up = (d_act * glu).astype(BF16)

    def to_weight(a, b):
        return jnp.einsum("eft,dt->efd", a, b, preferred_element_type=F32).astype(BF16)

    term = jnp.einsum("efd,eft->dt", w_gate, d_pre_gate, preferred_element_type=F32)
    term = term + jnp.einsum("efd,eft->dt", w_up, d_pre_up, preferred_element_type=F32)
    keep, other = swap_sum(term.astype(BF16))
    keep, other, act, d_pre_gate, d_pre_up = lax.optimization_barrier((keep, other, act, d_pre_gate, d_pre_up))
    own, arrived = plane_sum(keep, other, rows)
    d_gate, d_up, d_down = to_weight(d_pre_gate, x), to_weight(d_pre_up, x), to_weight(act, g)
    own, arrived, d_gate, d_up, d_down = lax.optimization_barrier((own, arrived, d_gate, d_up, d_down))
    for a in arrived:
        own = own + a.astype(F32)
    return ring_sum(own).T, d_gate, d_up, d_down


def solution(mesh):
    groups, shards = mesh.shape["expert"], mesh.shape["etp"]
    split = Mesh(mesh.devices.reshape(groups, shards // 2, 2), ("expert", "ring", "core"))
    etp = ("ring", "core")
    hidden = P("expert", etp, None)
    return jax.shard_map(
        body,
        mesh=split,
        in_specs=(P("expert", etp), P("expert", etp), P("expert", None), P("expert", None), hidden, hidden, hidden),
        out_specs=(P("expert", etp), hidden, hidden, hidden),
        check_vma=False,
    )
```

```python
import jax
import jax.numpy as jnp
from jax import lax
from jax.sharding import Mesh
from jax.sharding import PartitionSpec as P

BF16, F32 = jnp.bfloat16, jnp.float32


def xor_send(a, axis, s):
    return lax.ppermute(a, axis, [(i, i ^ s) for i in range(lax.axis_size(axis))])


def ring_order(stack):
    ring, bit = lax.axis_index("ring"), 1
    pieces = [stack[i] for i in range(stack.shape[0])]
    while bit < len(pieces):
        swap = (ring & bit) > 0
        pieces = [jnp.where(swap, pieces[i ^ bit], pieces[i]) for i in range(len(pieces))]
        bit *= 2
    return jnp.stack(pieces)


def ring_gather(own):
    return [own] + [xor_send(own, "ring", s) for s in range(1, lax.axis_size("ring"))]


def plane_gather(a):
    return [a] + [xor_send(a, "expert", s) for s in range(1, lax.axis_size("expert"))]


def both_cores(half):
    other = xor_send(half, "core", 1)
    half, other = lax.optimization_barrier((ring_order(half), other))
    other = ring_order(other)
    first = lax.axis_index("core") == 0
    both = jnp.where(first, jnp.stack([half, other], 1), jnp.stack([other, half], 1))
    return both.reshape(-1, both.shape[-1])


def at(a, i):
    return lax.dynamic_index_in_dim(a, i, 0, False)


def swap_sum(part):
    core = lax.axis_index("core")
    part = part.reshape(lax.axis_size("ring"), 2, -1, part.shape[-1])
    keep = lax.dynamic_index_in_dim(part, core, 1, False)
    give = lax.dynamic_index_in_dim(part, 1 - core, 1, False)
    return keep, xor_send(give, "core", 1)


def plane_sum(keep, other, rows):
    chip = keep.astype(F32) + other.astype(F32)
    far = chip[:, :, rows:].astype(BF16)
    arrived = [
        xor_send(far[:, :, (s - 1) * rows : s * rows], "expert", s)
        for s in range(1, lax.axis_size("expert"))
    ]
    return chip[:, :, :rows], arrived


def ring_sum(mine):
    ring = lax.axis_index("ring")
    mine_b = mine.astype(BF16)
    home = at(mine, ring)
    for s in range(1, lax.axis_size("ring")):
        home = home + xor_send(at(mine_b, ring ^ s), "ring", s).astype(F32)
    return home.astype(BF16)


def body(tokens, grad_out, gates, routes, w_gate, w_up, w_down):
    groups = lax.axis_size("expert")
    local = w_gate.shape[0]
    width, rows = tokens.shape[1], tokens.shape[0]
    group = lax.axis_index("expert")

    ids = jnp.arange(groups * local, dtype=jnp.int32)
    named = routes[None] == ids[:, None, None]
    weight = jnp.sum(jnp.where(named, gates[None], 0.0), -1)
    parts, left = [], weight
    for _ in range(3):
        part = lax.reduce_precision(left, 8, 7)
        parts.append(part.astype(BF16))
        left = left - part

    def to_hidden(w, a):
        return jnp.einsum("efd,dt->eft", w, a, preferred_element_type=F32)

    x_own, g_own = tokens.T, grad_out.T
    x_ring = ring_gather(x_own)
    early = plane_gather(jnp.concatenate([x_own, g_own] + parts, 0))
    early, g_first = lax.optimization_barrier((early, g_own))
    g_ring = ring_gather(g_first)

    def next_places(near):
        return xor_send(jnp.stack(near[1:]), "ring", 1)

    def all_places(near, nearer, ring_own, rest):
        rows = [jnp.concatenate(near, -1)]
        rows.append(jnp.concatenate([ring_own[1]] + [nearer[s] for s in range(groups - 1)], -1))
        rest = jnp.concatenate(rest, -1)
        return jnp.stack(rows + [rest[i] for i in range(rest.shape[0])])

    x_near = [a[:width] for a in early]
    g_near = [a[width : 2 * width] for a in early]
    x_next = next_places(x_near)
    x_ring = lax.optimization_barrier(x_ring)
    x_rest = plane_gather(jnp.stack(x_ring[2:]))
    g_ring, g_near, _, _ = lax.optimization_barrier((g_ring, g_near, x_rest, x_next))
    g_next = next_places(g_near)
    g_rest = plane_gather(jnp.stack(g_ring[2:]))
    x = both_cores(all_places(x_near, x_next, x_ring, x_rest))
    coef = jnp.concatenate([a[2 * width :] for a in early], -1).reshape(3, groups * local, -1).astype(F32)
    coef = lax.dynamic_slice_in_dim(coef[0] + coef[1] + coef[2], group * local, local, 0)[:, None, :]
    pre_gate = to_hidden(w_gate, x)
    pre_up = to_hidden(w_up, x)
    sig = jax.nn.sigmoid(1.702 * pre_gate)
    glu = pre_gate * sig
    act = (glu * (pre_up + 1.0) * coef).astype(BF16)
    slope = (pre_up + 1.0) * (sig + 1.702 * pre_gate * sig * (1.0 - sig))
    g_rest, g_next, act, glu, slope = lax.optimization_barrier((g_rest, g_next, act, glu, slope))
    g = both_cores(all_places(g_near, g_next, g_ring, g_rest))

    d_act = to_hidden(w_down, g) * coef
    d_pre_gate = (d_act * slope).astype(BF16)
    d_pre_up = (d_act * glu).astype(BF16)

    def to_weight(a, b):
        return jnp.einsum("eft,dt->efd", a, b, preferred_element_type=F32).astype(BF16)

    term = jnp.einsum("efd,eft->dt", w_gate, d_pre_gate, preferred_element_type=F32)
    term = term + jnp.einsum("efd,eft->dt", w_up, d_pre_up, preferred_element_type=F32)
    keep, other = swap_sum(term.astype(BF16))
    keep, other, act, d_pre_gate, d_pre_up = lax.optimization_barrier((keep, other, act, d_pre_gate, d_pre_up))
    own, arrived = plane_sum(keep, other, rows)
    d_gate, d_up, d_down = to_weight(d_pre_gate, x), to_weight(d_pre_up, x), to_weight(act, g)
    own, arrived, d_gate, d_up, d_down = lax.optimization_barrier((own, arrived, d_gate, d_up, d_down))
    for a in arrived:
        own = own + a.astype(F32)
    return ring_sum(own).T, d_gate, d_up, d_down


def solution(mesh):
    groups, shards = mesh.shape["expert"], mesh.shape["etp"]
    split = Mesh(mesh.devices.reshape(groups, shards // 2, 2), ("expert", "ring", "core"))
    etp = ("ring", "core")
    hidden = P("expert", etp, None)
    return jax.shard_map(
        body,
        mesh=split,
        in_specs=(P("expert", etp), P("expert", etp), P("expert", None), P("expert", None), hidden, hidden, hidden),
        out_specs=(P("expert", etp), hidden, hidden, hidden),
        check_vma=False,
    )
```

```python
import jax
import jax.numpy as jnp
from jax import lax
from jax.sharding import Mesh
from jax.sharding import PartitionSpec as P

BF16, F32 = jnp.bfloat16, jnp.float32


def xor_send(a, axis, s):
    return lax.ppermute(a, axis, [(i, i ^ s) for i in range(lax.axis_size(axis))])


def ring_order(stack):
    ring, bit = lax.axis_index("ring"), 1
    pieces = [stack[i] for i in range(stack.shape[0])]
    while bit < len(pieces):
        swap = (ring & bit) > 0
        pieces = [jnp.where(swap, pieces[i ^ bit], pieces[i]) for i in range(len(pieces))]
        bit *= 2
    return jnp.stack(pieces)


def ring_gather(own):
    sent = [xor_send(own, "ring", s) for s in range(lax.axis_size("ring") - 1, 0, -1)]
    return [own] + sent[::-1]


def plane_gather(a):
    sent = [xor_send(a, "expert", s) for s in range(lax.axis_size("expert") - 1, 0, -1)]
    return [a] + sent[::-1]


def both_cores(half):
    other = xor_send(half, "core", 1)
    half, other = lax.optimization_barrier((ring_order(half), other))
    other = ring_order(other)
    first = lax.axis_index("core") == 0
    both = jnp.where(first, jnp.stack([half, other], 1), jnp.stack([other, half], 1))
    return both.reshape(-1, both.shape[-1])


def at(a, i):
    return lax.dynamic_index_in_dim(a, i, 0, False)


def swap_sum(part):
    core = lax.axis_index("core")
    part = part.reshape(lax.axis_size("ring"), 2, -1, part.shape[-1])
    keep = lax.dynamic_index_in_dim(part, core, 1, False)
    give = lax.dynamic_index_in_dim(part, 1 - core, 1, False)
    return keep, xor_send(give, "core", 1)


def plane_out(a, rows):
    return [
        xor_send(a[..., s * rows : (s + 1) * rows], "expert", s)
        for s in range(lax.axis_size("expert") - 1, 0, -1)
    ]


def add_all(first, others):
    for a in others:
        first = first + a.astype(F32)
    return first


def body(tokens, grad_out, gates, routes, w_gate, w_up, w_down):
    groups = lax.axis_size("expert")
    local = w_gate.shape[0]
    width, rows = tokens.shape[1], tokens.shape[0]
    group = lax.axis_index("expert")

    ids = jnp.arange(groups * local, dtype=jnp.int32)
    named = routes[None] == ids[:, None, None]
    weight = jnp.sum(jnp.where(named, gates[None], 0.0), -1)
    parts, left = [], weight
    for _ in range(3):
        part = lax.reduce_precision(left, 8, 7)
        parts.append(part.astype(BF16))
        left = left - part

    def to_hidden(w, a):
        return jnp.einsum("efd,dt->eft", w, a, preferred_element_type=F32)

    x_own, g_own = tokens.T, grad_out.T
    x_ring = ring_gather(x_own)
    early = plane_gather(jnp.concatenate([x_own, g_own] + parts, 0))
    early, g_first = lax.optimization_barrier((early, g_own))
    g_ring = ring_gather(g_first)

    def next_places(near):
        return xor_send(jnp.stack(near[1:]), "ring", 1)

    def all_places(near, nearer, ring_own, rest):
        rows = [jnp.concatenate(near, -1)]
        rows.append(jnp.concatenate([ring_own[1]] + [nearer[s] for s in range(groups - 1)], -1))
        rest = jnp.concatenate(rest, -1)
        return jnp.stack(rows + [rest[i] for i in range(rest.shape[0])])

    x_near = [a[:width] for a in early]
    g_near = [a[width : 2 * width] for a in early]
    x_next = next_places(x_near)
    x_ring = lax.optimization_barrier(x_ring)
    x_rest = plane_gather(jnp.stack(x_ring[2:]))
    x_rest, x_next, g_ring, g_near = lax.optimization_barrier((x_rest, x_next, g_ring, g_near))
    g_next = next_places(g_near)
    g_rest = plane_gather(jnp.stack(g_ring[2:]))
    x = both_cores(all_places(x_near, x_next, x_ring, x_rest))
    coef = jnp.concatenate([a[2 * width :] for a in early], -1).reshape(3, groups * local, -1).astype(F32)
    coef = lax.dynamic_slice_in_dim(coef[0] + coef[1] + coef[2], group * local, local, 0)[:, None, :]
    pre_gate = to_hidden(w_gate, x)
    pre_up = to_hidden(w_up, x)
    sig = jax.nn.sigmoid(1.702 * pre_gate)
    glu = pre_gate * sig
    act = (glu * (pre_up + 1.0) * coef).astype(BF16)
    slope = (pre_up + 1.0) * (sig + 1.702 * pre_gate * sig * (1.0 - sig))
    g_rest, g_next, act, glu, slope = lax.optimization_barrier((g_rest, g_next, act, glu, slope))
    g = both_cores(all_places(g_near, g_next, g_ring, g_rest))

    d_act = to_hidden(w_down, g) * coef
    d_pre_gate = (d_act * slope).astype(BF16)
    d_pre_up = (d_act * glu).astype(BF16)

    def to_weight(a, b):
        return jnp.einsum("eft,dt->efd", a, b, preferred_element_type=F32).astype(BF16)

    term = jnp.einsum("efd,eft->dt", w_gate, d_pre_gate, preferred_element_type=F32)
    term = term + jnp.einsum("efd,eft->dt", w_up, d_pre_up, preferred_element_type=F32)
    keep, other = swap_sum(term.astype(BF16))
    keep, other, act, d_pre_gate, d_pre_up = lax.optimization_barrier((keep, other, act, d_pre_gate, d_pre_up))
    ring, rings = lax.axis_index("ring"), lax.axis_size("ring")

    def chip(s):
        return at(keep, ring ^ s).astype(F32) + at(other, ring ^ s).astype(F32)

    far = jnp.stack([chip(s) for s in range(2, rings)])
    far_in = plane_out(far.astype(BF16), rows)
    near_in = xor_send(chip(1).astype(BF16), "ring", 1)
    far_own, near = far[:, :, :rows], chip(0)
    d_gate, d_up = to_weight(d_pre_gate, x), to_weight(d_pre_up, x)
    far_own, far_in, near, near_in, d_gate, d_up, act = lax.optimization_barrier(
        (far_own, far_in, near, near_in, d_gate, d_up, act)
    )
    far_sum = add_all(far_own, far_in).astype(BF16)
    near = near + near_in.astype(F32)
    arrived = [xor_send(far_sum[s - 2], "ring", s) for s in range(rings - 1, 1, -1)]
    arrived += plane_out(near.astype(BF16), rows)
    own = near[:, :rows]
    d_down = to_weight(act, g)
    own, arrived, d_down = lax.optimization_barrier((own, arrived, d_down))
    return add_all(own, arrived).astype(BF16).T, d_gate, d_up, d_down


def solution(mesh):
    groups, shards = mesh.shape["expert"], mesh.shape["etp"]
    split = Mesh(mesh.devices.reshape(groups, shards // 2, 2), ("expert", "ring", "core"))
    etp = ("ring", "core")
    hidden = P("expert", etp, None)
    return jax.shard_map(
        body,
        mesh=split,
        in_specs=(P("expert", etp), P("expert", etp), P("expert", None), P("expert", None), hidden, hidden, hidden),
        out_specs=(P("expert", etp), hidden, hidden, hidden),
        check_vma=False,
    )
```

```python
import jax
import jax.numpy as jnp
from jax import lax
from jax.sharding import Mesh
from jax.sharding import PartitionSpec as P

BF16, F32 = jnp.bfloat16, jnp.float32


def xor_send(a, axis, s):
    return lax.ppermute(a, axis, [(i, i ^ s) for i in range(lax.axis_size(axis))])


def ring_order(stack):
    ring, bit = lax.axis_index("ring"), 1
    pieces = [stack[i] for i in range(stack.shape[0])]
    while bit < len(pieces):
        swap = (ring & bit) > 0
        pieces = [jnp.where(swap, pieces[i ^ bit], pieces[i]) for i in range(len(pieces))]
        bit *= 2
    return jnp.stack(pieces)


def ring_gather(own):
    sent = [xor_send(own, "ring", s) for s in range(lax.axis_size("ring") - 1, 0, -1)]
    return [own] + sent[::-1]


def plane_gather(a):
    sent = [xor_send(a, "expert", s) for s in range(lax.axis_size("expert") - 1, 0, -1)]
    return [a] + sent[::-1]


def both_cores(half):
    other = xor_send(half, "core", 1)
    half, other = lax.optimization_barrier((ring_order(half), other))
    other = ring_order(other)
    first = lax.axis_index("core") == 0
    both = jnp.where(first, jnp.stack([half, other], 1), jnp.stack([other, half], 1))
    return both.reshape(-1, both.shape[-1])


def at(a, i):
    return lax.dynamic_index_in_dim(a, i, 0, False)


def swap_sum(part):
    core = lax.axis_index("core")
    part = part.reshape(lax.axis_size("ring"), 2, -1, part.shape[-1])
    keep = lax.dynamic_index_in_dim(part, core, 1, False)
    give = lax.dynamic_index_in_dim(part, 1 - core, 1, False)
    return keep, xor_send(give, "core", 1)


def plane_out(a, rows):
    return [
        xor_send(a[..., s * rows : (s + 1) * rows], "expert", s)
        for s in range(lax.axis_size("expert") - 1, 0, -1)
    ]


def add_all(first, others):
    for a in others:
        first = first + a.astype(F32)
    return first


def body(tokens, grad_out, gates, routes, w_gate, w_up, w_down):
    groups = lax.axis_size("expert")
    local = w_gate.shape[0]
    width, rows = tokens.shape[1], tokens.shape[0]
    group = lax.axis_index("expert")

    ids = jnp.arange(groups * local, dtype=jnp.int32)
    named = routes[None] == ids[:, None, None]
    weight = jnp.sum(jnp.where(named, gates[None], 0.0), -1)
    parts, left = [], weight
    for _ in range(3):
        part = lax.reduce_precision(left, 8, 7)
        parts.append(part.astype(BF16))
        left = left - part

    def to_hidden(w, a):
        return jnp.einsum("efd,dt->eft", w, a, preferred_element_type=F32)

    x_own, g_own = tokens.T, grad_out.T
    x_ring = ring_gather(x_own)
    early = plane_gather(jnp.concatenate([x_own, g_own] + parts, 0))
    early[1], g_first = lax.optimization_barrier((early[1], g_own))
    g_ring = ring_gather(g_first)

    def next_places(near):
        return xor_send(jnp.stack(near[1:]), "ring", 1)

    def all_places(near, nearer, ring_own, rest):
        rows = [jnp.concatenate(near, -1)]
        rows.append(jnp.concatenate([ring_own[1]] + [nearer[s] for s in range(groups - 1)], -1))
        rest = jnp.concatenate(rest, -1)
        return jnp.stack(rows + [rest[i] for i in range(rest.shape[0])])

    x_near = [a[:width] for a in early]
    g_near = [a[width : 2 * width] for a in early]
    x_next = next_places(x_near)
    x_ring = lax.optimization_barrier(x_ring)
    x_rest = plane_gather(jnp.stack(x_ring[2:]))
    g_ring, g_near, x_rest[1], x_rest[-1] = lax.optimization_barrier((g_ring, g_near, x_rest[1], x_rest[-1]))
    g_next = next_places(g_near)
    g_rest = plane_gather(jnp.stack(g_ring[2:]))
    x = both_cores(all_places(x_near, x_next, x_ring, x_rest))
    coef = jnp.concatenate([a[2 * width :] for a in early], -1).reshape(3, groups * local, -1).astype(F32)
    coef = lax.dynamic_slice_in_dim(coef[0] + coef[1] + coef[2], group * local, local, 0)[:, None, :]
    pre_gate = to_hidden(w_gate, x)
    pre_up = to_hidden(w_up, x)
    sig = jax.nn.sigmoid(1.702 * pre_gate)
    glu = pre_gate * sig
    act = (glu * (pre_up + 1.0) * coef).astype(BF16)
    slope = (pre_up + 1.0) * (sig + 1.702 * pre_gate * sig * (1.0 - sig))
    g_rest, g_next, act, glu, slope = lax.optimization_barrier((g_rest, g_next, act, glu, slope))
    g = both_cores(all_places(g_near, g_next, g_ring, g_rest))

    d_act = to_hidden(w_down, g) * coef
    d_pre_gate = (d_act * slope).astype(BF16)
    d_pre_up = (d_act * glu).astype(BF16)

    def to_weight(a, b):
        return jnp.einsum("eft,dt->efd", a, b, preferred_element_type=F32).astype(BF16)

    term = jnp.einsum("efd,eft->dt", w_gate, d_pre_gate, preferred_element_type=F32)
    term = term + jnp.einsum("efd,eft->dt", w_up, d_pre_up, preferred_element_type=F32)
    keep, other = swap_sum(term.astype(BF16))
    keep, other, act, d_pre_gate, d_pre_up = lax.optimization_barrier((keep, other, act, d_pre_gate, d_pre_up))
    ring, rings = lax.axis_index("ring"), lax.axis_size("ring")

    def chip(s):
        return at(keep, ring ^ s).astype(F32) + at(other, ring ^ s).astype(F32)

    far = jnp.stack([chip(s) for s in range(2, rings)])
    far_in = plane_out(far.astype(BF16), rows)
    near_in = xor_send(chip(1).astype(BF16), "ring", 1)
    far_own, near = far[:, :, :rows], chip(0)
    d_gate, d_up = to_weight(d_pre_gate, x), to_weight(d_pre_up, x)
    far_own, far_in, near, near_in, d_gate, d_up, act = lax.optimization_barrier(
        (far_own, far_in, near, near_in, d_gate, d_up, act)
    )
    far_sum = add_all(far_own, far_in).astype(BF16)
    near = near + near_in.astype(F32)
    arrived = [xor_send(far_sum[s - 2], "ring", s) for s in range(rings - 1, 1, -1)]
    arrived += plane_out(near.astype(BF16), rows)
    own = near[:, :rows]
    d_down = to_weight(act, g)
    own, arrived, d_down = lax.optimization_barrier((own, arrived, d_down))
    return add_all(own, arrived).astype(BF16).T, d_gate, d_up, d_down


def solution(mesh):
    groups, shards = mesh.shape["expert"], mesh.shape["etp"]
    split = Mesh(mesh.devices.reshape(groups, shards // 2, 2), ("expert", "ring", "core"))
    etp = ("ring", "core")
    hidden = P("expert", etp, None)
    return jax.shard_map(
        body,
        mesh=split,
        in_specs=(P("expert", etp), P("expert", etp), P("expert", None), P("expert", None), hidden, hidden, hidden),
        out_specs=(P("expert", etp), hidden, hidden, hidden),
        check_vma=False,
    )
```

```python
import jax
import jax.numpy as jnp
from jax import lax
from jax.sharding import Mesh
from jax.sharding import PartitionSpec as P

BF16, F32 = jnp.bfloat16, jnp.float32


def xor_send(a, axis, s):
    return lax.ppermute(a, axis, [(i, i ^ s) for i in range(lax.axis_size(axis))])


def ring_order(stack):
    ring, bit = lax.axis_index("ring"), 1
    pieces = [stack[i] for i in range(stack.shape[0])]
    while bit < len(pieces):
        swap = (ring & bit) > 0
        pieces = [jnp.where(swap, pieces[i ^ bit], pieces[i]) for i in range(len(pieces))]
        bit *= 2
    return jnp.stack(pieces)


def ring_gather(own):
    sent = [xor_send(own, "ring", s) for s in range(lax.axis_size("ring") - 1, 0, -1)]
    return [own] + sent[::-1]


def plane_gather(a):
    sent = [xor_send(a, "expert", s) for s in range(lax.axis_size("expert") - 1, 0, -1)]
    return [a] + sent[::-1]


def both_cores(half):
    other = xor_send(half, "core", 1)
    half, other = lax.optimization_barrier((ring_order(half), other))
    other = ring_order(other)
    first = lax.axis_index("core") == 0
    both = jnp.where(first, jnp.stack([half, other], 1), jnp.stack([other, half], 1))
    return both.reshape(-1, both.shape[-1])


def at(a, i):
    return lax.dynamic_index_in_dim(a, i, 0, False)


def swap_sum(part):
    core = lax.axis_index("core")
    part = part.reshape(lax.axis_size("ring"), 2, -1, part.shape[-1])
    keep = lax.dynamic_index_in_dim(part, core, 1, False)
    give = lax.dynamic_index_in_dim(part, 1 - core, 1, False)
    return keep, xor_send(give, "core", 1)


def plane_out(a, rows):
    return [
        xor_send(a[..., s * rows : (s + 1) * rows], "expert", s)
        for s in range(lax.axis_size("expert") - 1, 0, -1)
    ]


def add_all(first, others):
    for a in others:
        first = first + a.astype(F32)
    return first


def body(tokens, grad_out, gates, routes, w_gate, w_up, w_down):
    groups = lax.axis_size("expert")
    local = w_gate.shape[0]
    width, rows = tokens.shape[1], tokens.shape[0]
    group = lax.axis_index("expert")

    ids = jnp.arange(groups * local, dtype=jnp.int32)
    named = routes[None] == ids[:, None, None]
    weight = jnp.sum(jnp.where(named, gates[None], 0.0), -1)
    parts, left = [], weight
    for _ in range(3):
        part = lax.reduce_precision(left, 8, 7)
        parts.append(part.astype(BF16))
        left = left - part

    def to_hidden(w, a):
        return jnp.einsum("efd,dt->eft", w, a, preferred_element_type=F32)

    x_own, g_own = tokens.T, grad_out.T
    x_ring = ring_gather(x_own)
    early = plane_gather(jnp.concatenate([x_own, g_own] + parts, 0))
    x_ring[1], g_first = lax.optimization_barrier((x_ring[1], g_own))
    g_ring = ring_gather(g_first)

    def next_places(near):
        return xor_send(jnp.stack(near[1:]), "ring", 1)

    def all_places(near, nearer, ring_own, rest):
        rows = [jnp.concatenate(near, -1)]
        rows.append(jnp.concatenate([ring_own[1]] + [nearer[s] for s in range(groups - 1)], -1))
        rest = jnp.concatenate(rest, -1)
        return jnp.stack(rows + [rest[i] for i in range(rest.shape[0])])

    x_near = [a[:width] for a in early]
    g_near = [a[width : 2 * width] for a in early]
    x_next = next_places(x_near)
    x_ring = lax.optimization_barrier(x_ring)
    x_rest = plane_gather(jnp.stack(x_ring[2:]))
    g_ring, g_near, x_rest[1], x_rest[-1] = lax.optimization_barrier((g_ring, g_near, x_rest[1], x_rest[-1]))
    g_next = next_places(g_near)
    g_rest = plane_gather(jnp.stack(g_ring[2:]))
    x = both_cores(all_places(x_near, x_next, x_ring, x_rest))
    coef = jnp.concatenate([a[2 * width :] for a in early], -1).reshape(3, groups * local, -1).astype(F32)
    coef = lax.dynamic_slice_in_dim(coef[0] + coef[1] + coef[2], group * local, local, 0)[:, None, :]
    pre_gate = to_hidden(w_gate, x)
    pre_up = to_hidden(w_up, x)
    sig = jax.nn.sigmoid(1.702 * pre_gate)
    glu = pre_gate * sig
    act = (glu * (pre_up + 1.0) * coef).astype(BF16)
    slope = (pre_up + 1.0) * (sig + 1.702 * pre_gate * sig * (1.0 - sig))
    g_rest, g_next, act, glu, slope = lax.optimization_barrier((g_rest, g_next, act, glu, slope))
    g = both_cores(all_places(g_near, g_next, g_ring, g_rest))

    d_act = to_hidden(w_down, g) * coef
    d_pre_gate = (d_act * slope).astype(BF16)
    d_pre_up = (d_act * glu).astype(BF16)

    def to_weight(a, b):
        return jnp.einsum("eft,dt->efd", a, b, preferred_element_type=F32).astype(BF16)

    term = jnp.einsum("efd,eft->dt", w_gate, d_pre_gate, preferred_element_type=F32)
    term = term + jnp.einsum("efd,eft->dt", w_up, d_pre_up, preferred_element_type=F32)
    keep, other = swap_sum(term.astype(BF16))
    keep, other, act, d_pre_gate, d_pre_up = lax.optimization_barrier((keep, other, act, d_pre_gate, d_pre_up))
    ring, rings = lax.axis_index("ring"), lax.axis_size("ring")

    def chip(s):
        return at(keep, ring ^ s).astype(F32) + at(other, ring ^ s).astype(F32)

    far = jnp.stack([chip(s) for s in range(2, rings)])
    far_in = plane_out(far.astype(BF16), rows)
    near_in = xor_send(chip(1).astype(BF16), "ring", 1)
    far_own, near = far[:, :, :rows], chip(0)
    d_gate, d_up = to_weight(d_pre_gate, x), to_weight(d_pre_up, x)
    far_own, far_in, near, near_in, d_gate, d_up, act = lax.optimization_barrier(
        (far_own, far_in, near, near_in, d_gate, d_up, act)
    )
    far_sum = add_all(far_own, far_in).astype(BF16)
    near = near + near_in.astype(F32)
    arrived = [xor_send(far_sum[s - 2], "ring", s) for s in range(rings - 1, 1, -1)]
    arrived += plane_out(near.astype(BF16), rows)
    own = near[:, :rows]
    d_down = to_weight(act, g)
    own, arrived, d_down = lax.optimization_barrier((own, arrived, d_down))
    return add_all(own, arrived).astype(BF16).T, d_gate, d_up, d_down


def solution(mesh):
    groups, shards = mesh.shape["expert"], mesh.shape["etp"]
    split = Mesh(mesh.devices.reshape(groups, shards // 2, 2), ("expert", "ring", "core"))
    etp = ("ring", "core")
    hidden = P("expert", etp, None)
    return jax.shard_map(
        body,
        mesh=split,
        in_specs=(P("expert", etp), P("expert", etp), P("expert", None), P("expert", None), hidden, hidden, hidden),
        out_specs=(P("expert", etp), hidden, hidden, hidden),
        check_vma=False,
    )
```
